32 devices in a mesh: groups: 2 (over x), ta: 16 (over z, y, core).
Axes of the slice: x: 2, y: 2, z: 4, core: 2. Of those that a mesh axis runs over, the one named last changes fastest.
Arguments:
- source: float32 [32, 4, 32, 256], P(('groups', 'ta')), parts along dimension 0, may hold values from -13 to 13
- links: float32 [16, 4, 9, 256, 256], P('ta'), may hold values from -0.046875 to 0.046875
- prolongator: float32 [16, 4, 16, 256], P('ta'), may hold values from -0.375 to 0.375
- coarse_inverse: float32 [1024, 1024], P('ta'), may hold values from -1 to 2
Outputs:
- solution: float32 [32, 4, 32, 256], P(('groups', 'ta')), parts along dimension 0
- residual: float32 [32, 4, 32, 256], P(('groups', 'ta')), parts along dimension 0
The draws below stay inside these ranges and needn't reach their ends.
There are 2 independent parts, one for each index of `groups`. The reference program is written for one: setup_inputs(seed, part) draws one part's arguments, and reference() takes and returns one part's arrays. A program takes and returns all parts, laid end to end along the dimension named above; an argument that names none is the same for every part. Nothing has to cross between parts.
All inputs are finite; a program needn't handle non-finite values.
Results may differ from the reference program's by a relative error of at most 0.0003.
Values sent between devices are 32-bit elements; how exact they have to be, the bound alone decides.
A program may use at most 64 MiB of HBM per device.

```python
import jax
import jax.numpy as jnp
from jax import lax

NC = 256
RHS = 32
LX = 1
LY = 2
LZ = 2
SWEEPS = 3
NT = 16
SP = 4
KS = 16
NCOARSE = 1024


def draw_source(key, part):
    noise_key = jax.random.fold_in(key, 11)
    noise = jnp.clip(jax.random.normal(noise_key, (NT, SP, RHS, NC), jnp.float32), -4.0, 4.0)
    ramped = 0.5 + jnp.arange(NT, dtype=jnp.float32) / max(NT - 1, 1)
    return noise * ramped[:, None, None, None]


def draw_coarse_inverse(key, part):
    noise_key = jax.random.fold_in(key, 21)
    spread = jnp.clip(jax.random.normal(noise_key, (NCOARSE, NCOARSE), jnp.float32), -4.0, 4.0)
    diagonal = jnp.ones((NCOARSE,), jnp.float32)
    return spread * NCOARSE ** (-0.5) + jnp.diag(diagonal)


def shard_levels(own_key, shape, pieces, low, largest):
    level = 1.0
    for axis_at, blocks in pieces:
        steps = jax.random.uniform(jax.random.fold_in(jax.random.fold_in(own_key, 6), axis_at), (blocks,), jnp.float32, low / len(pieces), largest / len(pieces))
        level = level * jnp.repeat(jnp.exp(steps), shape[axis_at] // blocks).reshape((-1,) + (1,) * (len(shape) - 1 - axis_at))
    return level


def bell_draw(own_key, extent, deviation, limit, pieces=(), held_as=jnp.bfloat16):
    loudness = shard_levels(own_key, extent, pieces, -0.22, 0.18) if pieces else 1.0
    entries = jax.random.normal(own_key, extent, jnp.float32) * deviation * loudness
    return jnp.minimum(jnp.maximum(entries, -limit), limit).astype(held_as)


def setup_inputs(seed: int = 0, part: int = 0) -> dict:
    splits = jax.random.split(jax.random.key(seed), 5)
    own_keys = jax.random.split(jax.random.fold_in(splits[4], part), 5)
    source = draw_source(jax.random.fold_in(jax.random.fold_in(splits[4], part), 71), part)
    links = bell_draw(splits[1], (NT, SP, 9, NC, NC), (0.12 * NC ** -0.5), 0.046875, ((0, 16),), jnp.float32)
    prolongator = bell_draw(splits[2], (NT, SP, KS, NC), NC ** -0.5, 0.375, ((0, 16),), jnp.float32)
    coarse_inverse = draw_coarse_inverse(jax.random.fold_in(splits[4], 71), part)
    return dict(source=source, links=links, prolongator=prolongator, coarse_inverse=coarse_inverse)


damping = 0.8
full_precision = lax.Precision.HIGHEST


def neighbours(field):
    grid = field.reshape(NT, LX, LY, LZ, RHS, NC)

    def rolled(amount, axis):
        return jnp.roll(grid, amount, axis).reshape(field.shape)

    return jnp.stack([field, rolled(-1, 0), rolled(1, 0), rolled(-1, 1), rolled(1, 1),
                      rolled(-1, 2), rolled(1, 2), rolled(-1, 3), rolled(1, 3)], axis=2)


def operate(links, field):
    return field + jnp.einsum("tsmab,tsmjb->tsja", links, neighbours(field),
                              precision=full_precision, preferred_element_type=jnp.float32)


def inner(first, second):
    return jnp.sum(first * second, axis=(0, 1, 3))


def smooth(links, solution, residual):
    for sweep in range(SWEEPS):
        image = operate(links, residual)
        factor = (damping * inner(image, residual) / inner(image, image))[:, None]
        solution = solution + factor * residual
        residual = residual - factor * image
    return solution, residual


def reference(source, links, prolongator, coarse_inverse):
    solution = jnp.zeros_like(source)
    residual = source
    solution, residual = smooth(links, solution, residual)
    restricted = jnp.einsum("tskc,tsjc->tskj", prolongator, residual,
                            precision=full_precision, preferred_element_type=jnp.float32).reshape(NCOARSE, RHS)
    coarse = jnp.dot(coarse_inverse, restricted, precision=full_precision, preferred_element_type=jnp.float32)
    correction = jnp.einsum("tskc,tskj->tsjc", prolongator, coarse.reshape(NT, SP, KS, RHS),
                            precision=full_precision, preferred_element_type=jnp.float32)
    image = operate(links, correction)
    factor = (inner(image, residual) / inner(image, image))[:, None]
    solution = solution + factor * correction
    residual = residual - factor * image
    solution, residual = smooth(links, solution, residual)
    return solution, residual
```

```python
import functools

import jax
import jax.numpy as jnp
from jax import lax
from jax.experimental import pallas as pl
from jax.experimental.pallas import tpu as pltpu
from jax.sharding import PartitionSpec as P

LINK_SUMS = ((0, 3, 4), (5, 6), (7, 8), (1,), (2,))
INNER_SUMS = 3
DAMPING = 0.8
SWEEPS = 3
STEP = 0.8
HIGHEST = lax.Precision.HIGHEST
F32 = jnp.float32
BF16 = jnp.bfloat16
GRAM_ROWS = 8


def dot(a, b):
    return jnp.dot(a, b, precision=HIGHEST, preferred_element_type=F32)


def kernel(
    n,
    source_ref,
    links_ref,
    prol_ref,
    inverse_ref,
    solution_ref,
    residual_ref,
    raw,
    lcat,
    weights,
    field,
    halo,
    acc,
    stage,
    gather,
    small_stage,
    small,
    rall,
    link_sem,
    halo_send,
    halo_recv,
    gather_send,
    gather_recv,
    small_send,
    small_recv,
):
    me = lax.axis_index("ta")
    sites, rhs, comps = source_ref.shape[1:]
    ks = prol_ref.shape[2]
    width = sites * rhs
    right, left = lax.rem(me + 1, n), lax.rem(me + n - 1, n)

    barrier = pltpu.get_barrier_semaphore()

    def greet(d, carry):
        pl.semaphore_signal(barrier, inc=1, device_id={"ta": lax.rem(me + d, n)})
        return carry

    lax.fori_loop(1, n, greet, 0)
    for s in range(sites):
        pltpu.make_async_copy(links_ref.at[0, s], raw.at[s], link_sem.at[s]).start()

    lane_site = lax.broadcasted_iota(jnp.int32, (1, width), 1) // rhs
    even = lane_site % 2 == 0

    def over_sites(x):
        shift = rhs
        while shift < width:
            x = x + pltpu.roll(x, shift, 1)
            shift *= 2
        return x

    prol = prol_ref[0].reshape(sites * ks, comps)
    row_site = lax.broadcasted_iota(jnp.int32, (sites * ks, width), 0) // ks
    diagonal = row_site == lax.broadcasted_iota(jnp.int32, (sites * ks, width), 1) // rhs

    def restrict(v):
        full = jnp.where(diagonal, dot(prol, v), 0.0)
        return functools.reduce(jnp.add, [full[s * ks : (s + 1) * ks] for s in range(sites)])

    def products(pairs):
        rows = [jnp.sum(a * b, axis=0, keepdims=True) for a, b in pairs]
        return jnp.concatenate(rows + [jnp.zeros((GRAM_ROWS - len(rows), width), F32)], axis=0)

    def halo_copies(r, f):
        out = []
        for side, to in ((0, left), (1, right)):
            out.append(
                pltpu.make_async_remote_copy(
                    src_ref=field.at[f],
                    dst_ref=halo.at[r, side],
                    send_sem=halo_send.at[r, side],
                    recv_sem=halo_recv.at[r, side],
                    device_id={"ta": to},
                )
            )
        return out

    sent = []

    def send_halo(r, f):
        copies = halo_copies(r, f)
        for c in copies:
            c.start()
        sent.extend(copies)
        return copies

    def exchange(k, value, staged, slots, send_sem, recv_sem):
        staged[k] = value
        slots[k, me] = value

        def one(d, carry):
            pltpu.make_async_remote_copy(
                src_ref=staged.at[k],
                dst_ref=slots.at[k, me],
                send_sem=send_sem.at[k],
                recv_sem=recv_sem.at[k],
                device_id={"ta": lax.rem(me + d, n)},
            ).start()
            return carry

        lax.fori_loop(1, n, one, 0)
        return pltpu.make_async_remote_copy(
            src_ref=slots.at[k, pl.ds(0, n - 1)],
            dst_ref=slots.at[k, pl.ds(0, n - 1)],
            send_sem=send_sem.at[k],
            recv_sem=recv_sem.at[k],
            device_id={"ta": right},
        )

    pending = []

    def exchange_large(k, value):
        c = exchange(k, value, stage, gather, gather_send, gather_recv)
        pending.append(c)
        return c

    def exchange_small(k, value):
        c = exchange(k, value, small_stage, small, small_send, small_recv)
        pending.append(c)
        return c

    def load_weights(at, v):
        hi = v.astype(BF16)
        lo = (v - hi.astype(F32)).astype(BF16)
        weights[at * comps : (at + 1) * comps, :width] = hi
        weights[at * comps : (at + 1) * comps, width:] = lo

    def multiply(lo_k, hi_k, add):
        def site(s, carry):
            p = jnp.dot(
                lcat[s, :, lo_k * comps : hi_k * comps],
                weights[lo_k * comps : hi_k * comps],
                preferred_element_type=F32,
            )
            z = p[:comps, :width] + p[:comps, width:] + p[comps:, :width]
            if add:
                acc[...] += jnp.where(lane_site == s, z, 0.0)
            else:
                acc[...] = jnp.where(lane_site == s, z, acc[...])
            return carry

        lax.fori_loop(0, sites, site, 0)

    def hop(r, f, shade=None):
        v = field[f]
        load_weights(0, v)
        load_weights(1, pltpu.roll(v, width // 2, 1))
        load_weights(2, jnp.where(even, pltpu.roll(v, width - rhs, 1), pltpu.roll(v, rhs, 1)))
        multiply(0, INNER_SUMS, False)
        copies = sent[-2:]
        for side, c in enumerate(copies):
            c.wait_recv()
            load_weights(INNER_SUMS + side, halo[r, side])
        multiply(INNER_SUMS, len(LINK_SUMS), True)
        return acc[...]

    def step(r, f, to):
        field[to] = (1.0 - STEP) * field[f] - STEP * hop(r, f)

    def sweeps(gram):
        c = [jnp.ones((1, width), F32)]
        x = [jnp.zeros((1, width), F32)] * SWEEPS
        for _ in range(SWEEPS):
            size = len(c)
            d = [(c[0]) / STEP] + [(c[i] - c[i - 1]) / STEP for i in range(1, size)] + [-c[-1] / STEP]
            gd = [
                functools.reduce(jnp.add, [gram(i, j) * d[j] for j in range(size + 1)])
                for i in range(size + 1)
            ]
            across = functools.reduce(jnp.add, [gd[i] * c[i] for i in range(size)])
            squared = functools.reduce(jnp.add, [gd[i] * d[i] for i in range(size + 1)])
            factor = DAMPING * across / squared
            x = [x[i] + factor * c[i] if i < size else x[i] for i in range(SWEEPS)]
            c = [c[i] - factor * d[i] if i < size else -factor * d[i] for i in range(size + 1)]
        return c, x

    def combine(coefficients, fields):
        return functools.reduce(jnp.add, [a * field[f] for a, f in zip(coefficients, fields)])

    field[0] = source_ref[0].reshape(width, comps).T
    pl.semaphore_wait(barrier, n - 1)
    send_halo(0, 0)

    def prepare(s, carry):
        pltpu.make_async_copy(links_ref.at[0, s], raw.at[s], link_sem.at[s]).wait()
        for at, members in enumerate(LINK_SUMS):
            total = functools.reduce(jnp.add, [raw[s, m] for m in members])
            hi = total.astype(BF16)
            lo = (total - hi.astype(F32)).astype(BF16)
            lcat[s, :comps, at * comps : (at + 1) * comps] = hi
            lcat[s, comps:, at * comps : (at + 1) * comps] = lo
        return carry

    lax.fori_loop(0, sites, prepare, 0)
    for k in range(SWEEPS + 1):
        if k:
            send_halo(k, k)
        value = jnp.concatenate(
            [restrict(field[k]), products([(field[k], field[i]) for i in range(k + 1)])], axis=0
        )
        exchange_large(k, value)
        step(k, k, k + 1)
    for k in range(SWEEPS + 1):
        pending[k].wait_recv()

    def total_of(slots, k, at):
        def one(t, total):
            return total + slots[k, t, at : at + GRAM_ROWS]

        return over_sites(lax.fori_loop(0, n, one, jnp.zeros((GRAM_ROWS, width), F32)))

    grams = [total_of(gather, k, ks) for k in range(SWEEPS + 1)]
    c, x = sweeps(lambda i, j: grams[max(i, j)][min(i, j) : min(i, j) + 1])

    def spread(t, carry):
        r = functools.reduce(jnp.add, [c[k] * gather[k, t, :ks] for k in range(SWEEPS + 1)])
        for s in range(sites):
            rall[pl.ds(pl.multiple_of((t * sites + s) * ks, ks), ks)] = jnp.where(
                lane_site == s, r, 0.0
            )
        return carry

    lax.fori_loop(0, n, spread, 0)
    coarse = over_sites(dot(inverse_ref[...], rall[...]))
    field[5] = dot(prol.T, jnp.where(diagonal, coarse, 0.0))
    send_halo(4, 5)
    residual = combine(c, range(SWEEPS + 1))
    field[7] = residual
    field[8] = combine(c, range(1, SWEEPS + 2))
    field[9] = combine(x, range(SWEEPS))
    field[6] = field[5] + hop(4, 5)
    send_halo(5, 6)
    exchange_small(0, products([(field[6], field[7]), (field[6], field[6])]))
    after = (1.0 - STEP) * field[6] - STEP * hop(5, 6)
    pending[-1].wait_recv()
    pair = total_of(small, 0, 0)
    g = pair[0:1] / pair[1:2]

    field[11] = field[8] - g * after
    send_halo(6, 11)
    field[10] = field[7] - g * field[6]
    field[9] = field[9] + g * field[5]
    step(6, 11, 12)
    send_halo(7, 12)
    early = [(i, j) for i in range(3) for j in range(i + 1)]
    late = [(3, j) for j in range(4)]
    exchange_small(1, products([(field[10 + i], field[10 + j]) for i, j in early]))
    step(7, 12, 13)
    exchange_small(2, products([(field[10 + i], field[10 + j]) for i, j in late]))
    pending[-2].wait_recv()
    pending[-1].wait_recv()
    sums = [total_of(small, 1, 0), total_of(small, 2, 0)]

    def gram(i, j):
        pair = (max(i, j), min(i, j))
        which = 0 if pair in early else 1
        row = (early, late)[which].index(pair)
        return sums[which][row : row + 1]

    c, x = sweeps(gram)
    residual_ref[0] = combine(c, range(10, 14)).T.reshape(sites, rhs, comps)
    solution_ref[0] = (field[9] + combine(x, range(10, 13))).T.reshape(sites, rhs, comps)
    for copy in sent + pending:
        copy.wait_send()


def local(source, links, prolongator, coarse_inverse):
    n = lax.axis_size("ta")
    _, sites, rhs, comps = source.shape
    ks = prolongator.shape[2]
    width = sites * rhs
    sums = len(LINK_SUMS)
    vmem = pl.BlockSpec(memory_space=pltpu.VMEM)
    dma = pltpu.SemaphoreType.DMA
    return pl.pallas_call(
        functools.partial(kernel, n),
        out_shape=(jax.ShapeDtypeStruct(source.shape, F32),) * 2,
        in_specs=[vmem, pl.BlockSpec(memory_space=pl.ANY), vmem, vmem],
        out_specs=(vmem, vmem),
        scratch_shapes=[
            pltpu.VMEM(links.shape[1:], F32),
            pltpu.VMEM((sites, 2 * comps, sums * comps), BF16),
            pltpu.VMEM((sums * comps, 2 * width), BF16),
            pltpu.VMEM((14, comps, width), F32),
            pltpu.VMEM((8, 2, comps, width), F32),
            pltpu.VMEM((comps, width), F32),
            pltpu.VMEM((SWEEPS + 1, ks + GRAM_ROWS, width), F32),
            pltpu.VMEM((SWEEPS + 1, n, ks + GRAM_ROWS, width), F32),
            pltpu.VMEM((3, GRAM_ROWS, width), F32),
            pltpu.VMEM((3, n, GRAM_ROWS, width), F32),
            pltpu.VMEM((n * sites * ks, width), F32),
            dma((sites,)),
            dma((8, 2)),
            dma((8, 2)),
            dma((SWEEPS + 1,)),
            dma((SWEEPS + 1,)),
            dma((3,)),
            dma((3,)),
        ],
        compiler_params=pltpu.CompilerParams(
            collective_id=0, has_side_effects=True, vmem_limit_bytes=60 * 1024 * 1024
        ),
    )(source, links, prolongator, coarse_inverse)


def solution(mesh):
    return jax.shard_map(
        local,
        mesh=mesh,
        in_specs=(
            P(("groups", "ta"), None, None, None),
            P("ta", None, None, None, None),
            P("ta", None, None, None),
            P("ta", None),
        ),
        out_specs=(P(("groups", "ta"), None, None, None), P(("groups", "ta"), None, None, None)),
        check_vma=False,
    )
```

```python
import functools

import jax
import jax.numpy as jnp
from jax import lax
from jax.experimental import pallas as pl
from jax.experimental.pallas import tpu as pltpu
from jax.sharding import PartitionSpec as P

LINK_SUMS = ((0, 3, 4), (5, 6), (7, 8), (1,), (2,))
INNER_SUMS = 3
DAMPING = 0.8
SWEEPS = 3
STEP = 0.8
HIGHEST = lax.Precision.HIGHEST
F32 = jnp.float32
BF16 = jnp.bfloat16
SMALL_ROWS = 2


def dot(a, b):
    return jnp.dot(a, b, precision=HIGHEST, preferred_element_type=F32)


def kernel(
    n,
    source_ref,
    links_ref,
    prol_ref,
    inverse_ref,
    solution_ref,
    residual_ref,
    raw,
    lcat,
    weights,
    field,
    outgoing,
    halo,
    prol_halo,
    coarse_out,
    coarse_halo,
    acc,
    stage,
    gather,
    small_stage,
    small,
    rall,
    link_sem,
    halo_send,
    halo_recv,
    near_send,
    near_recv,
    gather_send,
    gather_recv,
    small_send,
    small_recv,
):
    me = lax.axis_index("ta")
    sites, rhs, comps = source_ref.shape[1:]
    ks = prol_ref.shape[2]
    width = sites * rhs
    right, left = lax.rem(me + 1, n), lax.rem(me + n - 1, n)

    barrier = pltpu.get_barrier_semaphore()

    def greet(d, carry):
        pl.semaphore_signal(barrier, inc=1, device_id={"ta": lax.rem(me + d, n)})
        return carry

    lax.fori_loop(1, n, greet, 0)
    for s in range(sites):
        pltpu.make_async_copy(links_ref.at[0, s], raw.at[s], link_sem.at[s]).start()

    lane_site = lax.broadcasted_iota(jnp.int32, (1, width), 1) // rhs
    even = lane_site % 2 == 0

    def over_sites(x):
        shift = rhs
        while shift < width:
            x = x + pltpu.roll(x, shift, 1)
            shift *= 2
        return x

    prol = prol_ref[0].reshape(sites * ks, comps)
    row_site = lax.broadcasted_iota(jnp.int32, (sites * ks, width), 0) // ks
    diagonal = row_site == lax.broadcasted_iota(jnp.int32, (sites * ks, width), 1) // rhs

    def restrict(v):
        full = jnp.where(diagonal, dot(prol, v), 0.0)
        return functools.reduce(jnp.add, [full[s * ks : (s + 1) * ks] for s in range(sites)])

    def products(pairs, rows=1):
        packed = []
        for at in range(0, rows * sites, sites):
            row = jnp.zeros((1, width), F32)
            for i, (a, b) in enumerate(pairs[at : at + sites]):
                row = jnp.where(lane_site == i, over_sites(jnp.sum(a * b, axis=0, keepdims=True)), row)
            packed.append(row)
        return packed[0] if rows == 1 else jnp.concatenate(packed, axis=0)

    block = comps // sites

    def send_site(r, s, v):
        message = jnp.zeros((block, width), F32)
        for q in range(sites):
            moved = pltpu.roll(
                v[q * block : (q + 1) * block], lax.rem(q + sites - s, sites) * rhs, 1
            )
            message = jnp.where(lane_site == q, moved, message)
        outgoing[r, s] = message
        for side, to in ((0, left), (1, right)):
            pltpu.make_async_remote_copy(
                src_ref=outgoing.at[r, s],
                dst_ref=halo.at[r, side, s],
                send_sem=halo_send.at[r, side],
                recv_sem=halo_recv.at[r, side, s],
                device_id={"ta": to},
            ).start()

    def send_field(r, f):
        def one(s, carry):
            send_site(r, s, field[f])
            return carry

        lax.fori_loop(0, sites, one, 0)

    def near(k, src, dst):
        return [
            pltpu.make_async_remote_copy(
                src_ref=src,
                dst_ref=dst.at[side],
                send_sem=near_send.at[k, side],
                recv_sem=near_recv.at[k, side],
                device_id={"ta": to},
            )
            for side, to in ((0, left), (1, right))
        ]

    def exchange(k, value, staged, slots, send_sem, recv_sem):
        staged[k] = value
        slots[k, me] = value

        def one(d, carry):
            pltpu.make_async_remote_copy(
                src_ref=staged.at[k],
                dst_ref=slots.at[k, me],
                send_sem=send_sem.at[k],
                recv_sem=recv_sem.at[k],
                device_id={"ta": lax.rem(me + d, n)},
            ).start()
            return carry

        lax.fori_loop(1, n, one, 0)
        return pltpu.make_async_remote_copy(
            src_ref=slots.at[k, pl.ds(0, n - 1)],
            dst_ref=slots.at[k, pl.ds(0, n - 1)],
            send_sem=send_sem.at[k],
            recv_sem=recv_sem.at[k],
            device_id={"ta": right},
        )

    pending = []

    def exchange_large(k, value):
        c = exchange(k, value, stage, gather, gather_send, gather_recv)
        pending.append(c)
        return c

    def exchange_small(k, value):
        c = exchange(k, value, small_stage, small, small_send, small_recv)
        pending.append(c)
        return c

    def load_weights(at, v):
        hi = v.astype(BF16)
        lo = (v - hi.astype(F32)).astype(BF16)
        weights[at * comps : (at + 1) * comps, :width] = hi
        weights[at * comps : (at + 1) * comps, width:] = lo

    def product(s, lo_k, hi_k):
        p = jnp.dot(
            lcat[s, :, lo_k * comps : hi_k * comps],
            weights[lo_k * comps : hi_k * comps],
            preferred_element_type=F32,
        )
        return p[:comps, :width] + p[:comps, width:] + p[comps:, :width]

    def inner(f):
        v = field[f]
        load_weights(0, v)
        load_weights(1, pltpu.roll(v, width // 2, 1))
        load_weights(2, jnp.where(even, pltpu.roll(v, width - rhs, 1), pltpu.roll(v, rhs, 1)))

        def site(s, carry):
            acc[...] = jnp.where(lane_site == s, product(s, 0, INNER_SUMS), acc[...])
            return carry

        lax.fori_loop(0, sites, site, 0)

    def outer(r, f, to, of_field, of_links, send=None):
        def site(s, carry):
            if r is not None:
                for side in range(2):
                    pltpu.make_async_remote_copy(
                        src_ref=outgoing.at[r, s],
                        dst_ref=halo.at[r, side, s],
                        send_sem=halo_send.at[r, side],
                        recv_sem=halo_recv.at[r, side, s],
                        device_id={"ta": left},
                    ).wait_recv()
                    m = halo[r, side, s]
                    load_weights(
                        INNER_SUMS + side,
                        jnp.concatenate(
                            [
                                pltpu.roll(m, lax.rem(s + sites - q, sites) * rhs, 1)
                                for q in range(sites)
                            ],
                            axis=0,
                        ),
                    )
            new = of_field * field[f] + of_links * (acc[...] + product(s, INNER_SUMS, len(LINK_SUMS)))
            field[to] = jnp.where(lane_site == s, new, field[to])
            if send is not None:
                send_site(send, s, new)
            return carry

        lax.fori_loop(0, sites, site, 0)

    def sweeps(gram):
        c = [jnp.ones((1, width), F32)]
        x = [jnp.zeros((1, width), F32)] * SWEEPS
        for _ in range(SWEEPS):
            size = len(c)
            d = [(c[0]) / STEP] + [(c[i] - c[i - 1]) / STEP for i in range(1, size)] + [-c[-1] / STEP]
            gd = [
                functools.reduce(jnp.add, [gram(i, j) * d[j] for j in range(size + 1)])
                for i in range(size + 1)
            ]
            across = functools.reduce(jnp.add, [gd[i] * c[i] for i in range(size)])
            squared = functools.reduce(jnp.add, [gd[i] * d[i] for i in range(size + 1)])
            factor = DAMPING * across / squared
            x = [x[i] + factor * c[i] if i < size else x[i] for i in range(SWEEPS)]
            c = [c[i] - factor * d[i] if i < size else -factor * d[i] for i in range(size + 1)]
        return c, x

    def combine(coefficients, fields):
        return functools.reduce(jnp.add, [a * field[f] for a, f in zip(coefficients, fields)])

    field[0] = source_ref[0].reshape(width, comps).T
    pl.semaphore_wait(barrier, n - 1)
    send_field(0, 0)
    prol_copies = near(0, prol_ref.at[0], prol_halo)
    for copy in prol_copies:
        copy.start()

    def prepare(s, carry):
        pltpu.make_async_copy(links_ref.at[0, s], raw.at[s], link_sem.at[s]).wait()
        for at, members in enumerate(LINK_SUMS):
            total = functools.reduce(jnp.add, [raw[s, m] for m in members])
            hi = total.astype(BF16)
            lo = (total - hi.astype(F32)).astype(BF16)
            lcat[s, :comps, at * comps : (at + 1) * comps] = hi
            lcat[s, comps:, at * comps : (at + 1) * comps] = lo
        return carry

    lax.fori_loop(0, sites, prepare, 0)
    for k in range(SWEEPS + 1):
        value = jnp.concatenate(
            [restrict(field[k]), products([(field[k], field[i]) for i in range(k + 1)])], axis=0
        )
        exchange_large(k, value)
        inner(k)
        outer(k, k, k + 1, 1.0 - STEP, -STEP, k + 1 if k < SWEEPS else None)
    for k in range(SWEEPS + 1):
        pending[k].wait_recv()

    def total_of(slots, k, at, rows):
        def one(t, total):
            return total + slots[k, t, at : at + rows]

        return lax.fori_loop(0, n, one, jnp.zeros((rows, width), F32))

    def unpack(total, i):
        row = total[i // sites : i // sites + 1]
        return over_sites(jnp.where(lane_site == i % sites, row, 0.0))

    totals = [total_of(gather, k, ks, 1) for k in range(SWEEPS + 1)]
    grams = {(k, i): unpack(totals[k], i) for k in range(SWEEPS + 1) for i in range(k + 1)}
    c, x = sweeps(lambda i, j: grams[max(i, j), min(i, j)])

    def spread(t, carry):
        r = functools.reduce(jnp.add, [c[k] * gather[k, t, :ks] for k in range(SWEEPS + 1)])
        for s in range(sites):
            rall[pl.ds(pl.multiple_of((t * sites + s) * ks, ks), ks)] = jnp.where(
                lane_site == s, r, 0.0
            )
        return carry

    lax.fori_loop(0, n, spread, 0)
    coarse = over_sites(dot(inverse_ref[...], rall[...]))
    coarse = jnp.where(diagonal, coarse, 0.0)
    compact = functools.reduce(jnp.add, [coarse[s * ks : (s + 1) * ks] for s in range(sites)])
    coarse_out[...] = compact
    coarse_copies = near(1, coarse_out, coarse_halo)
    for copy in coarse_copies:
        copy.start()
    field[5] = dot(prol.T, coarse)
    inner(5)
    field[7] = combine(c, range(SWEEPS + 1))
    field[8] = combine(c, range(1, SWEEPS + 2))
    field[9] = combine(x, range(SWEEPS))
    for side in range(2):
        prol_copies[side].wait_recv()
        coarse_copies[side].wait_recv()
        there = jnp.where(diagonal, jnp.concatenate([coarse_halo[side]] * sites, axis=0), 0.0)
        vectors = prol_halo[side].reshape(sites * ks, comps)
        load_weights(INNER_SUMS + side, dot(vectors.T, there))
    outer(None, 5, 6, 1.0, 1.0, 4)
    exchange_small(0, products([(field[6], field[7]), (field[6], field[6])], SMALL_ROWS))
    inner(6)
    outer(4, 6, 14, 1.0 - STEP, -STEP)
    pending[-1].wait_recv()
    pair = total_of(small, 0, 0, SMALL_ROWS)
    g = unpack(pair, 0) / unpack(pair, 1)

    field[11] = field[8] - g * field[14]
    send_field(5, 11)
    field[10] = field[7] - g * field[6]
    field[9] = field[9] + g * field[5]
    inner(11)
    outer(5, 11, 12, 1.0 - STEP, -STEP, 6)
    early = [(i, j) for i in range(3) for j in range(i + 1)]
    late = [(3, j) for j in range(4)]
    exchange_small(1, products([(field[10 + i], field[10 + j]) for i, j in early], SMALL_ROWS))
    inner(12)
    outer(6, 12, 13, 1.0 - STEP, -STEP)
    exchange_small(2, products([(field[10 + i], field[10 + j]) for i, j in late], SMALL_ROWS))
    pending[-2].wait_recv()
    pending[-1].wait_recv()
    sums = [total_of(small, 1, 0, SMALL_ROWS), total_of(small, 2, 0, SMALL_ROWS)]
    grams_after = {pair: unpack(sums[0], early.index(pair)) for pair in early}
    grams_after.update({pair: unpack(sums[1], late.index(pair)) for pair in late})

    def gram(i, j):
        return grams_after[max(i, j), min(i, j)]

    c, x = sweeps(gram)
    residual_ref[0] = combine(c, range(10, 14)).T.reshape(sites, rhs, comps)
    solution_ref[0] = (field[9] + combine(x, range(10, 13))).T.reshape(sites, rhs, comps)
    for r in range(halo.shape[0]):
        for side in range(2):
            pltpu.make_async_remote_copy(
                src_ref=outgoing.at[r],
                dst_ref=halo.at[r, side],
                send_sem=halo_send.at[r, side],
                recv_sem=halo_recv.at[r, side, 0],
                device_id={"ta": left},
            ).wait_send()
    for copy in pending + prol_copies + coarse_copies:
        copy.wait_send()


def local(source, links, prolongator, coarse_inverse):
    n = lax.axis_size("ta")
    _, sites, rhs, comps = source.shape
    ks = prolongator.shape[2]
    width = sites * rhs
    sums = len(LINK_SUMS)
    vmem = pl.BlockSpec(memory_space=pltpu.VMEM)
    dma = pltpu.SemaphoreType.DMA
    return pl.pallas_call(
        functools.partial(kernel, n),
        out_shape=(jax.ShapeDtypeStruct(source.shape, F32),) * 2,
        in_specs=[vmem, pl.BlockSpec(memory_space=pl.ANY), vmem, vmem],
        out_specs=(vmem, vmem),
        scratch_shapes=[
            pltpu.VMEM(links.shape[1:], F32),
            pltpu.VMEM((sites, 2 * comps, sums * comps), BF16),
            pltpu.VMEM((sums * comps, 2 * width), BF16),
            pltpu.VMEM((15, comps, width), F32),
            pltpu.VMEM((7, sites, comps // sites, width), F32),
            pltpu.VMEM((7, 2, sites, comps // sites, width), F32),
            pltpu.VMEM((2, *prolongator.shape[1:]), F32),
            pltpu.VMEM((ks, width), F32),
            pltpu.VMEM((2, ks, width), F32),
            pltpu.VMEM((comps, width), F32),
            pltpu.VMEM((SWEEPS + 1, ks + 1, width), F32),
            pltpu.VMEM((SWEEPS + 1, n, ks + 1, width), F32),
            pltpu.VMEM((3, SMALL_ROWS, width), F32),
            pltpu.VMEM((3, n, SMALL_ROWS, width), F32),
            pltpu.VMEM((n * sites * ks, width), F32),
            dma((sites,)),
            dma((7, 2)),
            dma((7, 2, sites)),
            dma((2, 2)),
            dma((2, 2)),
            dma((SWEEPS + 1,)),
            dma((SWEEPS + 1,)),
            dma((3,)),
            dma((3,)),
        ],
        compiler_params=pltpu.CompilerParams(
            collective_id=0, has_side_effects=True, vmem_limit_bytes=60 * 1024 * 1024
        ),
    )(source, links, prolongator, coarse_inverse)


def solution(mesh):
    return jax.shard_map(
        local,
        mesh=mesh,
        in_specs=(
            P(("groups", "ta"), None, None, None),
            P("ta", None, None, None, None),
            P("ta", None, None, None),
            P("ta", None),
        ),
        out_specs=(P(("groups", "ta"), None, None, None), P(("groups", "ta"), None, None, None)),
        check_vma=False,
    )
```

```python
import functools

import jax
import jax.numpy as jnp
from jax import lax
from jax.experimental import pallas as pl
from jax.experimental.pallas import tpu as pltpu
from jax.sharding import PartitionSpec as P

LINK_SUMS = ((0, 3, 4), (5, 6), (7, 8), (1,), (2,))
INNER_SUMS = 3
DAMPING = 0.8
SWEEPS = 3
STEP = 0.8
HIGHEST = lax.Precision.HIGHEST
F32 = jnp.float32
BF16 = jnp.bfloat16
SMALL_ROWS = 2


def dot(a, b):
    return jnp.dot(a, b, precision=HIGHEST, preferred_element_type=F32)


def kernel(
    n,
    source_ref,
    links_ref,
    prol_ref,
    inverse_ref,
    solution_ref,
    residual_ref,
    raw,
    lcat,
    weights,
    field,
    outgoing,
    halo,
    prol_halo,
    coarse_out,
    coarse_halo,
    acc,
    stage,
    gather,
    small_stage,
    small,
    rall,
    link_sem,
    halo_send,
    halo_recv,
    near_send,
    near_recv,
    gather_send,
    gather_recv,
    small_send,
    small_recv,
):
    me = lax.axis_index("ta")
    sites, rhs, comps = source_ref.shape[1:]
    ks = prol_ref.shape[2]
    width = sites * rhs
    right, left = lax.rem(me + 1, n), lax.rem(me + n - 1, n)

    barrier = pltpu.get_barrier_semaphore()

    def greet(d, carry):
        pl.semaphore_signal(barrier, inc=1, device_id={"ta": lax.rem(me + d, n)})
        return carry

    lax.fori_loop(1, n, greet, 0)
    for s in range(sites):
        pltpu.make_async_copy(links_ref.at[0, s], raw.at[s], link_sem.at[s]).start()

    lane_site = lax.broadcasted_iota(jnp.int32, (1, width), 1) // rhs
    even = lane_site % 2 == 0

    def over_sites(x):
        shift = rhs
        while shift < width:
            x = x + pltpu.roll(x, shift, 1)
            shift *= 2
        return x

    prol = prol_ref[0].reshape(sites * ks, comps)
    row_site = lax.broadcasted_iota(jnp.int32, (sites * ks, width), 0) // ks
    diagonal = row_site == lax.broadcasted_iota(jnp.int32, (sites * ks, width), 1) // rhs

    def two_parts(a):
        hi = a.astype(BF16)
        return hi, (a - hi.astype(F32)).astype(BF16)

    prol_parts = jnp.concatenate(two_parts(prol), axis=0)
    inverse_parts = jnp.concatenate(two_parts(inverse_ref[...]), axis=0)

    def dot_parts(a, b):
        p = jnp.dot(a, b, preferred_element_type=F32)
        rows = a.shape[0] // 2
        return p[:rows, :width] + p[:rows, width:] + p[rows:, :width]

    def restrict():
        full = jnp.where(diagonal, dot_parts(prol_parts, weights[:comps]), 0.0)
        return functools.reduce(jnp.add, [full[s * ks : (s + 1) * ks] for s in range(sites)])

    def products(pairs, rows=1):
        packed = []
        for at in range(0, rows * sites, sites):
            row = jnp.zeros((1, width), F32)
            for i, (a, b) in enumerate(pairs[at : at + sites]):
                row = jnp.where(lane_site == i, over_sites(jnp.sum(a * b, axis=0, keepdims=True)), row)
            packed.append(row)
        return packed[0] if rows == 1 else jnp.concatenate(packed, axis=0)

    block = comps // sites

    def send_site(r, s, v):
        message = jnp.zeros((block, width), F32)
        for q in range(sites):
            moved = pltpu.roll(
                v[q * block : (q + 1) * block], lax.rem(q + sites - s, sites) * rhs, 1
            )
            message = jnp.where(lane_site == q, moved, message)
        outgoing[r, s] = message
        for side, to in ((0, left), (1, right)):
            pltpu.make_async_remote_copy(
                src_ref=outgoing.at[r, s],
                dst_ref=halo.at[r, side, s],
                send_sem=halo_send.at[r, side],
                recv_sem=halo_recv.at[r, side, s],
                device_id={"ta": to},
            ).start()

    def send_field(r, f):
        def one(s, carry):
            send_site(r, s, field[f])
            return carry

        lax.fori_loop(0, sites, one, 0)

    def near(k, src, dst):
        return [
            pltpu.make_async_remote_copy(
                src_ref=src,
                dst_ref=dst.at[side],
                send_sem=near_send.at[k, side],
                recv_sem=near_recv.at[k, side],
                device_id={"ta": to},
            )
            for side, to in ((0, left), (1, right))
        ]

    def exchange(k, value, staged, slots, send_sem, recv_sem):
        staged[k] = value
        slots[k, me] = value

        def one(d, carry):
            pltpu.make_async_remote_copy(
                src_ref=staged.at[k],
                dst_ref=slots.at[k, me],
                send_sem=send_sem.at[k],
                recv_sem=recv_sem.at[k],
                device_id={"ta": lax.rem(me + d, n)},
            ).start()
            return carry

        lax.fori_loop(1, n, one, 0)
        return pltpu.make_async_remote_copy(
            src_ref=slots.at[k, pl.ds(0, n - 1)],
            dst_ref=slots.at[k, pl.ds(0, n - 1)],
            send_sem=send_sem.at[k],
            recv_sem=recv_sem.at[k],
            device_id={"ta": right},
        )

    pending = []

    def exchange_large(k, value):
        c = exchange(k, value, stage, gather, gather_send, gather_recv)
        pending.append(c)
        return c

    def exchange_small(k, value):
        c = exchange(k, value, small_stage, small, small_send, small_recv)
        pending.append(c)
        return c

    def load_weights(at, v):
        hi = v.astype(BF16)
        lo = (v - hi.astype(F32)).astype(BF16)
        weights[at * comps : (at + 1) * comps, :width] = hi
        weights[at * comps : (at + 1) * comps, width:] = lo

    def product(s, lo_k, hi_k):
        k = slice(lo_k * comps, hi_k * comps)
        p = jnp.dot(lcat[s, :comps, k], weights[k], preferred_element_type=F32)
        q = jnp.dot(lcat[s, comps:, k], weights[k, :width], preferred_element_type=F32)
        return p[:, :width] + p[:, width:] + q

    def load_inner(f):
        v = field[f]
        load_weights(0, v)
        load_weights(1, pltpu.roll(v, width // 2, 1))
        load_weights(2, jnp.where(even, pltpu.roll(v, width - rhs, 1), pltpu.roll(v, rhs, 1)))

    def inner():
        def site(s, carry):
            acc[...] = jnp.where(lane_site == s, product(s, 0, INNER_SUMS), acc[...])
            return carry

        lax.fori_loop(0, sites, site, 0, unroll=True)

    def outer(r, f, to, of_field, of_links, send=None):
        def site(s, carry):
            if r is not None:
                for side in range(2):
                    pltpu.make_async_remote_copy(
                        src_ref=outgoing.at[r, s],
                        dst_ref=halo.at[r, side, s],
                        send_sem=halo_send.at[r, side],
                        recv_sem=halo_recv.at[r, side, s],
                        device_id={"ta": left},
                    ).wait_recv()
                    m = halo[r, side, s]
                    load_weights(
                        INNER_SUMS + side,
                        jnp.concatenate(
                            [
                                pltpu.roll(m, lax.rem(s + sites - q, sites) * rhs, 1)
                                for q in range(sites)
                            ],
                            axis=0,
                        ),
                    )
            new = of_field * field[f] + of_links * (acc[...] + product(s, INNER_SUMS, len(LINK_SUMS)))
            field[to] = jnp.where(lane_site == s, new, field[to])
            if send is not None:
                send_site(send, s, new)
            return carry

        lax.fori_loop(0, sites, site, 0)

    def sweeps(gram):
        c = [jnp.ones((1, width), F32)]
        x = [jnp.zeros((1, width), F32)] * SWEEPS
        for _ in range(SWEEPS):
            size = len(c)
            d = [(c[0]) / STEP] + [(c[i] - c[i - 1]) / STEP for i in range(1, size)] + [-c[-1] / STEP]
            gd = [
                functools.reduce(jnp.add, [gram(i, j) * d[j] for j in range(size + 1)])
                for i in range(size + 1)
            ]
            across = functools.reduce(jnp.add, [gd[i] * c[i] for i in range(size)])
            squared = functools.reduce(jnp.add, [gd[i] * d[i] for i in range(size + 1)])
            factor = DAMPING * across / squared
            x = [x[i] + factor * c[i] if i < size else x[i] for i in range(SWEEPS)]
            c = [c[i] - factor * d[i] if i < size else -factor * d[i] for i in range(size + 1)]
        return c, x

    def combine(coefficients, fields):
        return functools.reduce(jnp.add, [a * field[f] for a, f in zip(coefficients, fields)])

    field[0] = source_ref[0].reshape(width, comps).T
    pl.semaphore_wait(barrier, n - 1)
    send_field(0, 0)
    prol_copies = near(0, prol_ref.at[0], prol_halo)
    for copy in prol_copies:
        copy.start()

    def prepare(s, carry):
        pltpu.make_async_copy(links_ref.at[0, s], raw.at[s], link_sem.at[s]).wait()
        for at, members in enumerate(LINK_SUMS):
            total = functools.reduce(jnp.add, [raw[s, m] for m in members])
            hi = total.astype(BF16)
            lo = (total - hi.astype(F32)).astype(BF16)
            lcat[s, :comps, at * comps : (at + 1) * comps] = hi
            lcat[s, comps:, at * comps : (at + 1) * comps] = lo
        return carry

    lax.fori_loop(0, sites, prepare, 0)
    for k in range(SWEEPS + 1):
        load_inner(k)
        value = jnp.concatenate(
            [restrict(), products([(field[k], field[i]) for i in range(k + 1)])], axis=0
        )
        exchange_large(k, value)
        inner()
        outer(k, k, k + 1, 1.0 - STEP, -STEP, k + 1 if k < SWEEPS else None)
    for k in range(SWEEPS + 1):
        pending[k].wait_recv()

    def total_of(slots, k, at, rows):
        def one(t, total):
            return total + slots[k, t, at : at + rows]

        return lax.fori_loop(0, n, one, jnp.zeros((rows, width), F32))

    def unpack(total, i):
        row = total[i // sites : i // sites + 1]
        return over_sites(jnp.where(lane_site == i % sites, row, 0.0))

    totals = [total_of(gather, k, ks, 1) for k in range(SWEEPS + 1)]
    grams = {(k, i): unpack(totals[k], i) for k in range(SWEEPS + 1) for i in range(k + 1)}
    c, x = sweeps(lambda i, j: grams[max(i, j), min(i, j)])

    def spread(t, carry):
        r = functools.reduce(jnp.add, [c[k] * gather[k, t, :ks] for k in range(SWEEPS + 1)])
        for s in range(sites):
            hi, lo = two_parts(jnp.where(lane_site == s, r, 0.0))
            at = pl.ds(pl.multiple_of((t * sites + s) * ks, ks), ks)
            rall[at, :width] = hi
            rall[at, width:] = lo
        return carry

    lax.fori_loop(0, n, spread, 0)
    coarse = over_sites(dot_parts(inverse_parts, rall[...]))
    coarse = jnp.where(diagonal, coarse, 0.0)
    compact = functools.reduce(jnp.add, [coarse[s * ks : (s + 1) * ks] for s in range(sites)])
    coarse_out[...] = compact
    coarse_copies = near(1, coarse_out, coarse_halo)
    for copy in coarse_copies:
        copy.start()
    field[5] = dot(prol.T, coarse)
    load_inner(5)
    inner()
    field[7] = combine(c, range(SWEEPS + 1))
    field[8] = combine(c, range(1, SWEEPS + 2))
    field[9] = combine(x, range(SWEEPS))
    for side in range(2):
        prol_copies[side].wait_recv()
        coarse_copies[side].wait_recv()
        there = jnp.where(diagonal, jnp.concatenate([coarse_halo[side]] * sites, axis=0), 0.0)
        vectors = prol_halo[side].reshape(sites * ks, comps)
        load_weights(INNER_SUMS + side, dot(vectors.T, there))
    outer(None, 5, 6, 1.0, 1.0, 4)
    exchange_small(0, products([(field[6], field[7]), (field[6], field[6])], SMALL_ROWS))
    load_inner(6)
    inner()
    outer(4, 6, 14, 1.0 - STEP, -STEP)
    pending[-1].wait_recv()
    pair = total_of(small, 0, 0, SMALL_ROWS)
    g = unpack(pair, 0) / unpack(pair, 1)

    field[11] = field[8] - g * field[14]
    send_field(5, 11)
    field[10] = field[7] - g * field[6]
    field[9] = field[9] + g * field[5]
    load_inner(11)
    inner()
    outer(5, 11, 12, 1.0 - STEP, -STEP, 6)
    early = [(i, j) for i in range(3) for j in range(i + 1)]
    late = [(3, j) for j in range(4)]
    exchange_small(1, products([(field[10 + i], field[10 + j]) for i, j in early], SMALL_ROWS))
    load_inner(12)
    inner()
    outer(6, 12, 13, 1.0 - STEP, -STEP)
    exchange_small(2, products([(field[10 + i], field[10 + j]) for i, j in late], SMALL_ROWS))
    pending[-2].wait_recv()
    pending[-1].wait_recv()
    sums = [total_of(small, 1, 0, SMALL_ROWS), total_of(small, 2, 0, SMALL_ROWS)]
    grams_after = {pair: unpack(sums[0], early.index(pair)) for pair in early}
    grams_after.update({pair: unpack(sums[1], late.index(pair)) for pair in late})

    def gram(i, j):
        return grams_after[max(i, j), min(i, j)]

    c, x = sweeps(gram)
    residual_ref[...] = combine(c, range(10, 14))
    solution_ref[...] = field[9] + combine(x, range(10, 13))
    for r in range(halo.shape[0]):
        for side in range(2):
            pltpu.make_async_remote_copy(
                src_ref=outgoing.at[r],
                dst_ref=halo.at[r, side],
                send_sem=halo_send.at[r, side],
                recv_sem=halo_recv.at[r, side, 0],
                device_id={"ta": left},
            ).wait_send()
    for copy in pending + prol_copies + coarse_copies:
        copy.wait_send()


def turn(*refs):
    for column, row in zip(refs[:2], refs[2:]):
        row[0] = column[...].T.reshape(row.shape[1:])


def local(source, links, prolongator, coarse_inverse):
    n = lax.axis_size("ta")
    _, sites, rhs, comps = source.shape
    ks = prolongator.shape[2]
    width = sites * rhs
    sums = len(LINK_SUMS)
    vmem = pl.BlockSpec(memory_space=pltpu.VMEM)
    dma = pltpu.SemaphoreType.DMA
    columns = pl.pallas_call(
        functools.partial(kernel, n),
        out_shape=(jax.ShapeDtypeStruct((comps, width), F32),) * 2,
        in_specs=[vmem, pl.BlockSpec(memory_space=pl.ANY), vmem, vmem],
        out_specs=(vmem, vmem),
        scratch_shapes=[
            pltpu.VMEM(links.shape[1:], F32),
            pltpu.VMEM((sites, 2 * comps, sums * comps), BF16),
            pltpu.VMEM((sums * comps, 2 * width), BF16),
            pltpu.VMEM((15, comps, width), F32),
            pltpu.VMEM((7, sites, comps // sites, width), F32),
            pltpu.VMEM((7, 2, sites, comps // sites, width), F32),
            pltpu.VMEM((2, *prolongator.shape[1:]), F32),
            pltpu.VMEM((ks, width), F32),
            pltpu.VMEM((2, ks, width), F32),
            pltpu.VMEM((comps, width), F32),
            pltpu.VMEM((SWEEPS + 1, ks + 1, width), F32),
            pltpu.VMEM((SWEEPS + 1, n, ks + 1, width), F32),
            pltpu.VMEM((3, SMALL_ROWS, width), F32),
            pltpu.VMEM((3, n, SMALL_ROWS, width), F32),
            pltpu.VMEM((n * sites * ks, 2 * width), BF16),
            dma((sites,)),
            dma((7, 2)),
            dma((7, 2, sites)),
            dma((2, 2)),
            dma((2, 2)),
            dma((SWEEPS + 1,)),
            dma((SWEEPS + 1,)),
            dma((3,)),
            dma((3,)),
        ],
        compiler_params=pltpu.CompilerParams(
            collective_id=0, has_side_effects=True, vmem_limit_bytes=60 * 1024 * 1024
        ),
    )(source, links, prolongator, coarse_inverse)
    return pl.pallas_call(
        turn,
        out_shape=(jax.ShapeDtypeStruct(source.shape, F32),) * 2,
        in_specs=[vmem, vmem],
        out_specs=(vmem, vmem),
    )(*columns)


def solution(mesh):
    return jax.shard_map(
        local,
        mesh=mesh,
        in_specs=(
            P(("groups", "ta"), None, None, None),
            P("ta", None, None, None, None),
            P("ta", None, None, None),
            P("ta", None),
        ),
        out_specs=(P(("groups", "ta"), None, None, None), P(("groups", "ta"), None, None, None)),
        check_vma=False,
    )
```
